32 devices in a mesh: rows: 8 (over z, core), feat: 4 (over y, x).
Axes of the slice: x: 2, y: 2, z: 4, core: 2. Of those that a mesh axis runs over, the one named last changes fastest.
Arguments:
- features: float32 [8192, 2048], P('rows', 'feat'), may hold values from -200 to 200
- targets: float32 [8192, 2048], P('rows', 'feat'), may hold values from -2000 to 2000
Outputs:
- coefficients: float32 [2048, 2048], P('feat')
- residual: float32 [8192, 2048], P('rows', 'feat')
The draws below stay inside these ranges and needn't reach their ends.
All inputs are finite; a program needn't handle non-finite values.
Results may differ from the reference program's by a relative error of at most 0.0003.
Values sent between devices are 32-bit elements; how exact they have to be, the bound alone decides.
A program may use at most 64 MiB of HBM per device.

```python
import jax
import jax.numpy as jnp
from jax import lax

B = 512
TGT = 2048
SWEEPS = 1
NBLK = 4
ROWS = 8192
FEATS = 2048
TG = 512


def joint_draw(key):
    k_mix = jax.random.fold_in(key, 11)
    k_col = jax.random.fold_in(key, 12)
    k_true = jax.random.fold_in(key, 14)
    k_noise = jax.random.fold_in(key, 15)
    base = jax.random.normal(k_mix, (ROWS, FEATS), jnp.float32)
    mixed = base + 0.7 * jnp.roll(base, -(B // 2), axis=1)
    col_scale = jnp.exp(jax.random.uniform(k_col, (FEATS,), jnp.float32, 0.0, jnp.log(4.0)))
    data = jnp.clip(mixed * col_scale[None, :], -200.0, 200.0)
    truth = 0.1 * jax.random.normal(k_true, (FEATS, TGT), jnp.float32)
    noise = jax.random.normal(k_noise, (ROWS, TGT), jnp.float32)
    rhs = jnp.dot(data, truth, precision=lax.Precision.HIGHEST) + noise
    return (data, jnp.clip(rhs, -2000.0, 2000.0))


def draw_features(key, part):
    return joint_draw(key)[0]


def draw_targets(key, part):
    return joint_draw(key)[1]


def setup_inputs(seed: int = 0) -> dict:
    key_list = jax.random.split(jax.random.key(seed), 3)
    return {
        "features": draw_features(jax.random.fold_in(key_list[2], 71), 0),
        "targets": draw_targets(jax.random.fold_in(key_list[2], 71), 0),
    }


def reference(features, targets):
    hi = lax.Precision.HIGHEST

    def block_factor(j):
        block = lax.dynamic_slice_in_dim(features, j * B, B, 1)
        gram = lax.dot_general(block.astype(jnp.float32), block.astype(jnp.float32), (((0,), (0,)), ((), ())), precision=hi, preferred_element_type=jnp.float32)
        return jnp.linalg.cholesky(gram)
    lowers = lax.map(block_factor, jnp.arange(NBLK, dtype=jnp.int32))

    def one_group(group):
        start_res = lax.dynamic_slice_in_dim(targets, group * TG, TG, 1)
        coef = jnp.zeros((FEATS, TG), jnp.float32)

        def section(s, carry):
            coef, res = carry
            j = ((group + s) % NBLK).astype(jnp.int32)
            block = lax.dynamic_slice_in_dim(features, j * B, B, 1)
            product = lax.dot_general(block.astype(jnp.float32), res.astype(jnp.float32), (((0,), (0,)), ((), ())), precision=hi, preferred_element_type=jnp.float32)
            lower = lowers[j]
            step = jax.scipy.linalg.cho_solve((lower, True), product)
            old = lax.dynamic_slice_in_dim(coef, j * B, B, 0)
            coef = lax.dynamic_update_slice_in_dim(coef, old + step, j * B, 0)
            res = res - jnp.dot(block.astype(jnp.float32), step.astype(jnp.float32), precision=hi, preferred_element_type=jnp.float32)
            return (coef, res)
        return lax.fori_loop(0, SWEEPS * NBLK, section, (coef, start_res))
    coefs, residuals = lax.map(one_group, jnp.arange(NBLK, dtype=jnp.int32))
    coefficients = jnp.transpose(coefs, (1, 0, 2)).reshape(FEATS, TGT)
    residual = jnp.transpose(residuals, (1, 0, 2)).reshape(ROWS, TGT)
    return (coefficients, residual)
```

```python
import functools

import jax
import jax.numpy as jnp
from jax import lax
from jax.experimental import pallas as pl
from jax.experimental.pallas import tpu as pltpu
from jax.sharding import PartitionSpec as P

SWEEPS = 1
HI = lax.Precision.HIGHEST
GATHER_BYTES = 16 * 2**20


def shifted(block, axis, distance):
    devices = range(lax.axis_size(axis))
    route = [((i - distance) % len(devices), i) for i in devices]
    return lax.ppermute(block, axis, route)


def invert_tile(m):
    n = m.shape[0]
    lane = lax.broadcasted_iota(jnp.int32, (8, n), 1)
    sub = lax.broadcasted_iota(jnp.int32, (8, n), 0)
    lanes = lax.broadcasted_iota(jnp.int32, (n, n), 1)
    for q in range(n // 8):
        c = 8 * q
        panel = m[c : c + 8, :]
        d = [jnp.broadcast_to(panel[:, c + t : c + t + 1], (8, n)) for t in range(8)]
        mine = (lane >= c) & (lane < c + 8)
        panel = jnp.where(mine, jnp.where(lane - c == sub, 1.0, 0.0), panel)
        for t in range(8):
            inv = 1.0 / d[t][t : t + 1, :]
            row = panel[t : t + 1, :] * inv
            panel = jnp.where(sub == t, row, panel - d[t] * row)
            for u in range(t + 1, 8):
                head = d[u][t : t + 1, :] * inv
                d[u] = jnp.where(sub == t, head, d[u] - d[t] * head)
        new = jnp.where((lanes >= c) & (lanes < c + 8), 0.0, m)
        for t in range(8):
            new = new - jnp.broadcast_to(m[:, c + t : c + t + 1], (n, n)) * panel[t : t + 1, :]
        parts = [new[:c, :]] if q else []
        parts.append(panel)
        if c + 8 < n:
            parts.append(new[c + 8 :, :])
        m = jnp.concatenate(parts, axis=0)
    return m


def invert_kernel(tile, a_ref, o_ref):
    n = a_ref.shape[0]
    o_ref[...] = a_ref[...]
    eye = jnp.where(
        lax.broadcasted_iota(jnp.int32, (tile, tile), 0)
        == lax.broadcasted_iota(jnp.int32, (tile, tile), 1),
        1.0,
        0.0,
    )

    def block(k, _):
        at = pl.ds(pl.multiple_of(k * tile, tile), tile)
        pivot = invert_tile(o_ref[at, at])
        column = o_ref[:, at]
        o_ref[at, at] = eye
        row = jnp.dot(pivot, o_ref[at, :], precision=HI, preferred_element_type=jnp.float32)
        o_ref[:, at] = jnp.zeros((n, tile), jnp.float32)
        o_ref[...] -= jnp.dot(column, row, precision=HI, preferred_element_type=jnp.float32)
        o_ref[at, :] = row
        return 0

    lax.fori_loop(0, n // tile, block, 0)


def invert(gram):
    n = gram.shape[0]
    return pl.pallas_call(
        functools.partial(invert_kernel, min(128, n)),
        out_shape=jax.ShapeDtypeStruct((n, n), jnp.float32),
        in_specs=[pl.BlockSpec(memory_space=pltpu.VMEM)],
        out_specs=pl.BlockSpec(memory_space=pltpu.VMEM),
        cost_estimate=pl.CostEstimate(
            flops=2 * n**3 * 20, bytes_accessed=8 * n * n, transcendentals=0
        ),
    )(gram)


def tmul(a, b, precision):
    return lax.dot_general(
        a, b, (((0,), (0,)), ((), ())), precision=precision, preferred_element_type=jnp.float32
    )


def gathered(features, targets):
    high = lax.Precision.HIGH
    nblocks = lax.axis_size("feat")
    owner = lax.axis_index("feat")
    width = features.shape[1]
    group_width = targets.shape[1]
    gram = lax.psum(tmul(features, features, HI), "rows")
    blocks = [features] + [shifted(features, "feat", -s) for s in range(1, nblocks)]
    inverse = invert(gram)
    inverses = [inverse] + [shifted(inverse, "feat", -s) for s in range(1, nblocks)]
    res = targets
    coef = jnp.zeros((width, group_width * nblocks), jnp.float32)
    for s in range(nblocks):
        product = tmul(blocks[s], res, high)
        share = lax.psum_scatter(product, "rows", scatter_dimension=1, tiled=True)
        part = jnp.dot(inverses[s], share, precision=HI, preferred_element_type=jnp.float32)
        step = lax.all_gather(part, "rows", axis=1, tiled=True)
        res = res - jnp.dot(blocks[s], step, precision=high, preferred_element_type=jnp.float32)
        back = shifted(step, "feat", s) if s else step
        start = ((owner - s) % nblocks) * group_width
        coef = lax.dynamic_update_slice_in_dim(coef, back, start, 1)
    return (coef, res)


def general(features, targets):
    nblocks = lax.axis_size("feat")
    owner = lax.axis_index("feat")
    width = features.shape[1]
    group_width = targets.shape[1]
    inverse = invert(lax.psum(tmul(features, features, HI), "rows"))
    coef = jnp.zeros((width, group_width * nblocks), jnp.float32)

    def section(s, carry):
        coef, res = carry
        group = (owner - s) % nblocks
        product = tmul(features, res, HI)
        share = lax.psum_scatter(product, "rows", scatter_dimension=1, tiled=True)
        part = jnp.dot(inverse, share, precision=HI, preferred_element_type=jnp.float32)
        step = lax.all_gather(part, "rows", axis=1, tiled=True)
        start = group * group_width
        old = lax.dynamic_slice_in_dim(coef, start, group_width, 1)
        coef = lax.dynamic_update_slice_in_dim(coef, old + step, start, 1)
        res = res - jnp.dot(features, step, precision=HI, preferred_element_type=jnp.float32)
        res = shifted(res, "feat", 1)
        return (coef, res)

    return lax.fori_loop(0, SWEEPS * nblocks, section, (coef, targets))


def on_device(features, targets):
    nblocks = lax.axis_size("feat")
    if SWEEPS == 1 and nblocks * features.size * 4 <= GATHER_BYTES:
        return gathered(features, targets)
    return general(features, targets)


def solution(mesh):
    return jax.shard_map(
        on_device,
        mesh=mesh,
        in_specs=(P("rows", "feat"), P("rows", "feat")),
        out_specs=(P("feat", None), P("rows", "feat")),
        check_vma=False,
    )
```

```python
import functools

import jax
import jax.numpy as jnp
from jax import lax
from jax.experimental import pallas as pl
from jax.experimental.pallas import tpu as pltpu
from jax.sharding import PartitionSpec as P

SWEEPS = 1
HI = lax.Precision.HIGHEST
GATHER_BYTES = 16 * 2**20


def shifted(block, axis, distance):
    devices = range(lax.axis_size(axis))
    route = [((i - distance) % len(devices), i) for i in devices]
    return lax.ppermute(block, axis, route)


def invert_tile(m):
    n = m.shape[0]
    lane = lax.broadcasted_iota(jnp.int32, (8, n), 1)
    sub = lax.broadcasted_iota(jnp.int32, (8, n), 0)
    lanes = lax.broadcasted_iota(jnp.int32, (n, n), 1)
    for q in range(n // 8):
        c = 8 * q
        panel = m[c : c + 8, :]
        d = [jnp.broadcast_to(panel[:, c + t : c + t + 1], (8, n)) for t in range(8)]
        mine = (lane >= c) & (lane < c + 8)
        panel = jnp.where(mine, jnp.where(lane - c == sub, 1.0, 0.0), panel)
        for t in range(8):
            inv = 1.0 / d[t][t : t + 1, :]
            row = panel[t : t + 1, :] * inv
            panel = jnp.where(sub == t, row, panel - d[t] * row)
            for u in range(t + 1, 8):
                head = d[u][t : t + 1, :] * inv
                d[u] = jnp.where(sub == t, head, d[u] - d[t] * head)
        new = jnp.where((lanes >= c) & (lanes < c + 8), 0.0, m)
        for t in range(8):
            new = new - jnp.broadcast_to(m[:, c + t : c + t + 1], (n, n)) * panel[t : t + 1, :]
        parts = [new[:c, :]] if q else []
        parts.append(panel)
        if c + 8 < n:
            parts.append(new[c + 8 :, :])
        m = jnp.concatenate(parts, axis=0)
    return m


def invert_kernel(tile, a_ref, o_ref):
    n = a_ref.shape[0]
    o_ref[...] = a_ref[...]
    eye = jnp.where(
        lax.broadcasted_iota(jnp.int32, (tile, tile), 0)
        == lax.broadcasted_iota(jnp.int32, (tile, tile), 1),
        1.0,
        0.0,
    )

    def block(k, _):
        at = pl.ds(pl.multiple_of(k * tile, tile), tile)
        pivot = invert_tile(o_ref[at, at])
        column = o_ref[:, at]
        o_ref[at, at] = eye
        row = jnp.dot(pivot, o_ref[at, :], precision=HI, preferred_element_type=jnp.float32)
        o_ref[:, at] = jnp.zeros((n, tile), jnp.float32)
        o_ref[...] -= jnp.dot(column, row, precision=HI, preferred_element_type=jnp.float32)
        o_ref[at, :] = row
        return 0

    lax.fori_loop(0, n // tile, block, 0)


def invert(gram):
    n = gram.shape[0]
    return pl.pallas_call(
        functools.partial(invert_kernel, min(128, n)),
        out_shape=jax.ShapeDtypeStruct((n, n), jnp.float32),
        in_specs=[pl.BlockSpec(memory_space=pltpu.VMEM)],
        out_specs=pl.BlockSpec(memory_space=pltpu.VMEM),
        cost_estimate=pl.CostEstimate(
            flops=2 * n**3 * 20, bytes_accessed=8 * n * n, transcendentals=0
        ),
    )(gram)


def tmul(a, b, precision):
    return lax.dot_general(
        a, b, (((0,), (0,)), ((), ())), precision=precision, preferred_element_type=jnp.float32
    )


def split(x):
    high = x.astype(jnp.bfloat16)
    return high, (x - high.astype(jnp.float32)).astype(jnp.bfloat16)


def dot3(a, b, contract):
    dims = (contract, ((), ()))
    mul = functools.partial(
        lax.dot_general, dimension_numbers=dims, preferred_element_type=jnp.float32
    )
    return mul(a[0], b[0]) + (mul(a[0], b[1]) + mul(a[1], b[0]))


def sweep_kernel(
    nb, nrows, x_ref, t_ref, gram_ref, coef_ref, out_ref,
    xbuf, xh, xl, rest, ginv, part, gpart, gpair, grs, gfull, pairb, rsb, full, cbuf,
    fsem, psem, rsem, asem, wsem, isem, jsem, csem, dsem,
):
    r, g = lax.axis_index("rows"), lax.axis_index("feat")
    nz = nrows // 2
    z, c = r // 2, r % 2
    width, tg = x_ref.shape[1], t_ref.shape[1]
    mate = (r + 1 - 2 * c, g)

    def along(d):
        return (((z + d) % nz) * 2 + c, g)

    def owner_of(s):
        return (r, (g + s) % nb)

    def remote(src, dst, sems, at, device):
        return pltpu.make_async_remote_copy(
            src_ref=src, dst_ref=dst, send_sem=sems.at[(0,) + at], recv_sem=sems.at[(1,) + at],
            device_id=device, device_id_type=pl.DeviceIdType.MESH,
        )

    def rows_of(start, size):
        return pl.ds(pl.multiple_of(start, 8), size)

    barrier = pltpu.get_barrier_semaphore()
    peers = [mate] + [along(d) for d in range(1, nz)] + [owner_of(s) for s in range(1, nb)]
    for peer in peers:
        pl.semaphore_signal(barrier, inc=1, device_id=peer, device_id_type=pl.DeviceIdType.MESH)
    pl.semaphore_wait(barrier, len(peers))

    def block_copy(s):
        return remote(x_ref, xbuf.at[s - 1], fsem, (s - 1,), owner_of(nb - s))

    def all_reduce(k, n, src, pair_buf, rs_buf, dst, second, finish):
        half, size = n // 2, n // 2 // nz
        swap = remote(src.at[rows_of((1 - c) * half, half)], pair_buf, psem, (k,), mate)
        swap.start()
        second()
        swap.wait_recv()
        sends = [swap]
        for d in range(1, nz):
            slot = ((z + d) % nz) * size
            at = rows_of(c * half + slot, size)
            src[at, :] += pair_buf[rows_of(slot, size), :]
            copy = remote(src.at[at], rs_buf.at[d - 1], rsem, (k, d - 1), along(d))
            copy.start()
            sends.append(copy)
        total = src[rows_of(c * half + z * size, size), :] + pair_buf[rows_of(z * size, size), :]
        for d in range(1, nz):
            sends[d].wait_recv()
            total = total + rs_buf[d - 1]
        own = dst.at[rows_of(c * half + z * size, size)]
        own[...] = finish(total)
        spread = []
        for d in range(1, nz):
            copy = remote(own, own, asem, (k, d - 1), along(d))
            copy.start()
            spread.append(copy)
        relay = [remote(own, own, wsem, (k, 0), mate)]
        relay[0].start()
        for d in range(1, nz):
            spread[d - 1].wait_recv()
            piece = dst.at[rows_of(c * half + ((z - d + nz) % nz) * size, size)]
            relay.append(remote(piece, piece, wsem, (k, d), mate))
            relay[d].start()
        for copy in relay:
            copy.wait_recv()
        for copy in sends + spread + relay:
            copy.wait_send()

    def tiles(count, body):
        lax.fori_loop(0, count, lambda i, _: (body(i), 0)[1], 0)

    gpart[...] = gram_ref[...]
    tile = 128

    def turn(i):
        at = pl.ds(pl.multiple_of(i * tile, tile), tile)
        rest[at, :] = t_ref[:, at].T

    def start_blocks():
        for s in range(1, nb):
            block_copy(s).start()
        tiles(tg // tile, turn)

    all_reduce(0, width, gpart, gpair, grs, gfull, start_blocks, lambda v: v)
    invert_kernel(min(128, width), gfull, ginv.at[0])

    wh = width // 2
    mine = pl.ds(pl.multiple_of(c * wh, wh), wh)

    def inverse_copy(s):
        return remote(
            ginv.at[0, mine], ginv.at[s, mine], isem, (s - 1,), owner_of(nb - s)
        )

    def inverse_relay(s):
        return remote(ginv.at[s, mine], ginv.at[s, mine], jsem, (s - 1,), mate)

    for s in range(1, nb):
        inverse_copy(s).start()

    def columns(group):
        return pl.ds(pl.multiple_of(group * tg, tg), tg)

    def coef_copy(s):
        return remote(
            cbuf.at[s - 1], coef_ref.at[mine, columns(g)], csem, (s - 1,), owner_of(s)
        )

    def coef_relay(s):
        piece = coef_ref.at[mine, columns((g - s + nb) % nb)]
        return remote(piece, piece, dsem, (s - 1,), mate)

    for s in range(nb):
        if s:
            inverse_copy(s).wait_recv()
            inverse_relay(s).start()
            block_copy(s).wait_recv()
        block = xbuf.at[s - 1] if s else x_ref

        def cut(i):
            at = pl.ds(pl.multiple_of(i * tile, tile), tile)
            xh[at, :], xl[at, :] = split(block[at, :])

        tiles(block.shape[0] // tile, cut)

        def product(side):
            def body(i):
                at = rows_of(side * (tg // 2) + i * (tg // 4), tg // 4)
                part[at, :] = dot3(split(rest[at, :]), (xh[...], xl[...]), ((1,), (0,)))

            tiles(2, body)

        product(1 - c)

        def solve(total):
            if s:
                inverse_relay(s).wait_recv()
            return jnp.dot(total, ginv[s], precision=HI, preferred_element_type=jnp.float32)

        all_reduce(
            s + 1, tg, part, pairb.at[s], rsb.at[s], full.at[s], lambda: product(c), solve
        )
        step = full.at[s]
        if s:
            cbuf[s - 1] = step[:, mine].T
            coef_copy(s).start()
        else:
            coef_ref[:, columns(g)] = step[...].T
        if s > 1:
            coef_copy(s - 1).wait_recv()
            coef_relay(s - 1).start()

        def update(i):
            at = rows_of(i * (tg // 4), tg // 4)
            rest[at, :] -= dot3(split(step[at, :]), (xh[...], xl[...]), ((1,), (1,)))

        tiles(4, update)

    def turn_back(i):
        at = pl.ds(pl.multiple_of(i * tile, tile), tile)
        out_ref[:, at] = rest[at, :].T

    tiles(tg // tile, turn_back)
    if nb > 1:
        coef_copy(nb - 1).wait_recv()
        coef_relay(nb - 1).start()
    for s in range(1, nb):
        coef_relay(s).wait_recv()
    for s in range(1, nb):
        for copy in (block_copy, inverse_copy, inverse_relay, coef_copy, coef_relay):
            copy(s).wait_send()


def gathered(features, targets):
    nb, nrows = lax.axis_size("feat"), lax.axis_size("rows")
    height, width = features.shape
    tg = targets.shape[1]
    nz = nrows // 2
    f32 = jnp.float32
    gram = tmul(features, features, HI)
    vmem = pl.BlockSpec(memory_space=pltpu.VMEM)
    dma = pltpu.SemaphoreType.DMA
    return pl.pallas_call(
        functools.partial(sweep_kernel, nb, nrows),
        out_shape=(
            jax.ShapeDtypeStruct((width, tg * nb), f32),
            jax.ShapeDtypeStruct((height, tg), f32),
        ),
        in_specs=[vmem] * 3,
        out_specs=(vmem, vmem),
        scratch_shapes=[
            pltpu.VMEM((nb - 1, height, width), f32),
            pltpu.VMEM((height, width), jnp.bfloat16),
            pltpu.VMEM((height, width), jnp.bfloat16),
            pltpu.VMEM((tg, height), f32),
            pltpu.VMEM((nb, width, width), f32),
            pltpu.VMEM((tg, width), f32),
            pltpu.VMEM((width, width), f32),
            pltpu.VMEM((width // 2, width), f32),
            pltpu.VMEM((nz - 1, width // nrows, width), f32),
            pltpu.VMEM((width, width), f32),
            pltpu.VMEM((nb, tg // 2, width), f32),
            pltpu.VMEM((nb, nz - 1, tg // nrows, width), f32),
            pltpu.VMEM((nb, tg, width), f32),
            pltpu.VMEM((nb - 1, width // 2, tg), f32),
            dma((2, nb - 1)),
            dma((2, nb + 1)),
            dma((2, nb + 1, nz - 1)),
            dma((2, nb + 1, nz - 1)),
            dma((2, nb + 1, nz)),
            dma((2, nb - 1)),
            dma((2, nb - 1)),
            dma((2, nb - 1)),
            dma((2, nb - 1)),
        ],
        compiler_params=pltpu.CompilerParams(collective_id=0, has_side_effects=True),
    )(features, targets, gram)


def general(features, targets):
    nblocks = lax.axis_size("feat")
    owner = lax.axis_index("feat")
    width = features.shape[1]
    group_width = targets.shape[1]
    inverse = invert(lax.psum(tmul(features, features, HI), "rows"))
    coef = jnp.zeros((width, group_width * nblocks), jnp.float32)

    def section(s, carry):
        coef, res = carry
        group = (owner - s) % nblocks
        product = tmul(features, res, HI)
        share = lax.psum_scatter(product, "rows", scatter_dimension=1, tiled=True)
        part = jnp.dot(inverse, share, precision=HI, preferred_element_type=jnp.float32)
        step = lax.all_gather(part, "rows", axis=1, tiled=True)
        start = group * group_width
        old = lax.dynamic_slice_in_dim(coef, start, group_width, 1)
        coef = lax.dynamic_update_slice_in_dim(coef, old + step, start, 1)
        res = res - jnp.dot(features, step, precision=HI, preferred_element_type=jnp.float32)
        res = shifted(res, "feat", 1)
        return (coef, res)

    return lax.fori_loop(0, SWEEPS * nblocks, section, (coef, targets))


def on_device(features, targets):
    nblocks = lax.axis_size("feat")
    nrows = lax.axis_size("rows")
    width, group_width = features.shape[1], targets.shape[1]
    fits = nblocks > 1 and nblocks * features.size * 4 <= GATHER_BYTES
    whole = nrows % 2 == 0 and nrows > 2 and features.shape[0] % 128 == 0
    even = width % max(256, 8 * nrows) == 0 and group_width % max(128, 8 * nrows) == 0
    if SWEEPS == 1 and fits and whole and even:
        return gathered(features, targets)
    return general(features, targets)


def solution(mesh):
    return jax.shard_map(
        on_device,
        mesh=mesh,
        in_specs=(P("rows", "feat"), P("rows", "feat")),
        out_specs=(P("feat", None), P("rows", "feat")),
        check_vma=False,
    )
```

```python
import functools

import jax
import jax.numpy as jnp
from jax import lax
from jax.experimental import pallas as pl
from jax.experimental.pallas import tpu as pltpu
from jax.sharding import PartitionSpec as P

SWEEPS = 1
HI = lax.Precision.HIGHEST
GATHER_BYTES = 16 * 2**20


def shifted(block, axis, distance):
    devices = range(lax.axis_size(axis))
    route = [((i - distance) % len(devices), i) for i in devices]
    return lax.ppermute(block, axis, route)


def invert_tile(m):
    n = m.shape[0]
    lane = lax.broadcasted_iota(jnp.int32, (8, n), 1)
    sub = lax.broadcasted_iota(jnp.int32, (8, n), 0)
    lanes = lax.broadcasted_iota(jnp.int32, (n, n), 1)
    for q in range(n // 8):
        c = 8 * q
        panel = m[c : c + 8, :]
        d = [jnp.broadcast_to(panel[:, c + t : c + t + 1], (8, n)) for t in range(8)]
        mine = (lane >= c) & (lane < c + 8)
        panel = jnp.where(mine, jnp.where(lane - c == sub, 1.0, 0.0), panel)
        for t in range(8):
            inv = 1.0 / d[t][t : t + 1, :]
            row = panel[t : t + 1, :] * inv
            panel = jnp.where(sub == t, row, panel - d[t] * row)
            for u in range(t + 1, 8):
                head = d[u][t : t + 1, :] * inv
                d[u] = jnp.where(sub == t, head, d[u] - d[t] * head)
        new = jnp.where((lanes >= c) & (lanes < c + 8), 0.0, m)
        for t in range(8):
            new = new - jnp.broadcast_to(m[:, c + t : c + t + 1], (n, n)) * panel[t : t + 1, :]
        parts = [new[:c, :]] if q else []
        parts.append(panel)
        if c + 8 < n:
            parts.append(new[c + 8 :, :])
        m = jnp.concatenate(parts, axis=0)
    return m


def invert_kernel(tile, a_ref, o_ref):
    n = a_ref.shape[0]
    o_ref[...] = a_ref[...]
    eye = jnp.where(
        lax.broadcasted_iota(jnp.int32, (tile, tile), 0)
        == lax.broadcasted_iota(jnp.int32, (tile, tile), 1),
        1.0,
        0.0,
    )

    def block(k, _):
        at = pl.ds(pl.multiple_of(k * tile, tile), tile)
        pivot = invert_tile(o_ref[at, at])
        column = o_ref[:, at]
        o_ref[at, at] = eye
        row = jnp.dot(pivot, o_ref[at, :], precision=HI, preferred_element_type=jnp.float32)
        o_ref[:, at] = jnp.zeros((n, tile), jnp.float32)
        o_ref[...] -= jnp.dot(column, row, precision=HI, preferred_element_type=jnp.float32)
        o_ref[at, :] = row
        return 0

    lax.fori_loop(0, n // tile, block, 0)


def invert(gram):
    n = gram.shape[0]
    return pl.pallas_call(
        functools.partial(invert_kernel, min(128, n)),
        out_shape=jax.ShapeDtypeStruct((n, n), jnp.float32),
        in_specs=[pl.BlockSpec(memory_space=pltpu.VMEM)],
        out_specs=pl.BlockSpec(memory_space=pltpu.VMEM),
        cost_estimate=pl.CostEstimate(
            flops=2 * n**3 * 20, bytes_accessed=8 * n * n, transcendentals=0
        ),
    )(gram)


def tmul(a, b, precision):
    return lax.dot_general(
        a, b, (((0,), (0,)), ((), ())), precision=precision, preferred_element_type=jnp.float32
    )


def split(x):
    high = x.astype(jnp.bfloat16)
    return high, (x - high.astype(jnp.float32)).astype(jnp.bfloat16)


def dot3(a, b, contract):
    dims = (contract, ((), ()))
    mul = functools.partial(
        lax.dot_general, dimension_numbers=dims, preferred_element_type=jnp.float32
    )
    return mul(a[0], b[0]) + (mul(a[0], b[1]) + mul(a[1], b[0]))


class RowSum:
    def __init__(self, net, k, n, src, pair_buf, rs_buf, dst):
        self.net, self.k, self.src, self.dst = net, k, src, dst
        self.pair_buf, self.rs_buf = pair_buf, rs_buf
        self.half, self.size = n // 2, n // 2 // net.nz

    def slot(self, d):
        net = self.net
        return rows_of(net.c * self.half + ((net.z + d) % net.nz) * self.size, self.size)

    def pair_slot(self, d):
        return rows_of(((self.net.z + d) % self.net.nz) * self.size, self.size)

    def swap(self):
        net = self.net
        away = self.src.at[rows_of((1 - net.c) * self.half, self.half)]
        self.sends = [net.copy(away, self.pair_buf, net.psem, (self.k,), net.mate)]
        self.sends[0].start()

    def scatter(self):
        net = self.net
        self.sends[0].wait_recv()
        for d in range(1, net.nz):
            at = self.slot(d)
            self.src[at, :] += self.pair_buf[self.pair_slot(d), :]
            copy = net.copy(
                self.src.at[at], self.rs_buf.at[d - 1], net.rsem, (self.k, d - 1), net.along(d)
            )
            copy.start()
            self.sends.append(copy)

    def finish(self, apply):
        net = self.net
        total = self.src[self.slot(0), :] + self.pair_buf[self.pair_slot(0), :]
        for d in range(1, net.nz):
            self.sends[d].wait_recv()
            total = total + self.rs_buf[d - 1]
        own = self.dst.at[self.slot(0)]
        own[...] = apply(total)
        self.spread = []
        for d in range(1, net.nz):
            copy = net.copy(own, own, net.asem, (self.k, d - 1), net.along(d))
            copy.start()
            self.spread.append(copy)
        self.relay = [net.copy(own, own, net.wsem, (self.k, 0), net.mate)]
        self.relay[0].start()

    def collect(self):
        net = self.net
        for d in range(1, net.nz):
            self.spread[d - 1].wait_recv()
            piece = self.dst.at[self.slot(net.nz - d)]
            self.relay.append(net.copy(piece, piece, net.wsem, (self.k, d), net.mate))
            self.relay[d].start()
        for copy in self.relay:
            copy.wait_recv()
        for copy in self.sends + self.spread + self.relay:
            copy.wait_send()


class Net:
    def __init__(self, nb, nrows, psem, rsem, asem, wsem):
        self.nb, self.nz = nb, nrows // 2
        self.r, self.g = lax.axis_index("rows"), lax.axis_index("feat")
        self.z, self.c = self.r // 2, self.r % 2
        self.mate = (self.r + 1 - 2 * self.c, self.g)
        self.psem, self.rsem, self.asem, self.wsem = psem, rsem, asem, wsem

    def along(self, d):
        return (((self.z + d) % self.nz) * 2 + self.c, self.g)

    def owner_of(self, s):
        return (self.r, (self.g + s) % self.nb)

    def copy(self, src, dst, sems, at, device):
        return pltpu.make_async_remote_copy(
            src_ref=src, dst_ref=dst, send_sem=sems.at[(0,) + at], recv_sem=sems.at[(1,) + at],
            device_id=device, device_id_type=pl.DeviceIdType.MESH,
        )

    def greet(self):
        barrier = pltpu.get_barrier_semaphore()
        peers = [self.mate] + [self.along(d) for d in range(1, self.nz)]
        peers += [self.owner_of(s) for s in range(1, self.nb)]
        for peer in peers:
            pl.semaphore_signal(
                barrier, inc=1, device_id=peer, device_id_type=pl.DeviceIdType.MESH
            )
        pl.semaphore_wait(barrier, len(peers))


def rows_of(start, size):
    return pl.ds(pl.multiple_of(start, 8), size)


def tiles(count, body):
    lax.fori_loop(0, count, lambda i, _: (body(i), 0)[1], 0)


TILE = 128
CHUNKS = 2


def sweep_kernel(
    nb, nrows, x_ref, t_ref, coef_ref, out_ref,
    xbuf, xh, xl, rest, ginv, part, xt, gpart, gpair, grs, gsum, gfull, pairb, rsb, full, cbuf,
    fsem, psem, rsem, asem, wsem, isem, jsem, csem, dsem,
):
    net = Net(nb, nrows, psem, rsem, asem, wsem)
    c, g = net.c, net.g
    height, width = x_ref.shape
    tg = t_ref.shape[1]
    chunk = tg // CHUNKS
    net.greet()

    def block_copy(s):
        return net.copy(x_ref, xbuf.at[s - 1], fsem, (s - 1,), net.owner_of(nb - s))

    block_copy(1).start()

    m = width // TILE
    pairs = [(i, j) for i in range(m) for j in range(i + 1)]
    for i in range(m):
        xt[...] = x_ref[:, i * TILE : (i + 1) * TILE].T
        low = jnp.dot(
            xt[...], x_ref[:, : (i + 1) * TILE], precision=HI, preferred_element_type=jnp.float32
        )
        for j in range(i + 1):
            at = pairs.index((i, j)) * TILE
            gpart[at : at + TILE, :] = low[:, j * TILE : (j + 1) * TILE]
    gram = RowSum(net, 0, len(pairs) * TILE, gpart, gpair, grs, gsum)
    gram.swap()

    def turn(i):
        at = pl.ds(pl.multiple_of(i * TILE, TILE), TILE)
        rest[at, :] = t_ref[:, at].T

    def cut(s):
        block = xbuf.at[s - 1] if s else x_ref

        def body(i):
            at = pl.ds(pl.multiple_of(i * TILE, TILE), TILE)
            xh[s % 2, at, :], xl[s % 2, at, :] = split(block[at, :])

        tiles(height // TILE, body)

    sums = [
        [
            RowSum(
                net, 1 + s * CHUNKS + p, chunk, part.at[p], pairb.at[s, p], rsb.at[s, p],
                full.at[s, p],
            )
            for p in range(CHUNKS)
        ]
        for s in range(nb)
    ]

    def product(s, p, side):
        size = chunk // 2
        res = split(rest[rows_of(p * chunk + side * size, size), :])
        part[p, rows_of(side * size, size), :] = dot3(
            res, (xh[s % 2], xl[s % 2]), ((1,), (0,))
        )

    def update(s, p):
        def body(i):
            size = chunk // 2
            at = rows_of(i * size, size)
            step = split(full[s, p, at, :])
            rest[rows_of(p * chunk + i * size, size), :] -= dot3(
                step, (xh[s % 2], xl[s % 2]), ((1,), (1,))
            )

        tiles(2, body)

    gram.scatter()
    tiles(tg // TILE, turn)
    cut(0)
    gram.finish(lambda v: v)
    for p in range(CHUNKS):
        product(0, p, 1 - c)
        product(0, p, c)
    gram.collect()
    if nb > 2:
        block_copy(2).start()
    for p in range(CHUNKS):
        sums[0][p].swap()
    for p in range(CHUNKS):
        sums[0][p].scatter()
    for at, (i, j) in enumerate(pairs):
        tile = gsum[at * TILE : (at + 1) * TILE, :]
        gfull[i * TILE : (i + 1) * TILE, j * TILE : (j + 1) * TILE] = tile
        if i != j:
            gfull[j * TILE : (j + 1) * TILE, i * TILE : (i + 1) * TILE] = tile.T
    invert_kernel(TILE, gfull, ginv.at[0])

    wh = width // 2
    mine = pl.ds(pl.multiple_of(c * wh, wh), wh)

    def inverse_copy(s):
        return net.copy(
            ginv.at[0, mine], ginv.at[s, mine], isem, (s - 1,), net.owner_of(nb - s)
        )

    def inverse_relay(s):
        return net.copy(ginv.at[s, mine], ginv.at[s, mine], jsem, (s - 1,), net.mate)

    for s in range(1, nb):
        inverse_copy(s).start()
    for s in range(3, nb):
        block_copy(s).start()

    def columns(group, p):
        return pl.ds(pl.multiple_of(group * tg + p * chunk, chunk), chunk)

    def coef_copy(s, p):
        return net.copy(
            cbuf.at[s - 1, p], coef_ref.at[mine, columns(g, p)], csem, (s - 1, p),
            net.owner_of(s),
        )

    def coef_relay(s, p):
        piece = coef_ref.at[mine, columns((g - s + nb) % nb, p)]
        return net.copy(piece, piece, dsem, (s - 1, p), net.mate)

    def hand_over(s, p):
        if s:
            cbuf[s - 1, p] = full[s, p, :, mine].T
            coef_copy(s, p).start()
        else:
            coef_ref[:, columns(g, p)] = full[s, p].T

    for s in range(nb):
        last = s + 1 == nb
        if s:
            inverse_relay(s).wait_recv()
        for p in range(CHUNKS):
            sums[s][p].finish(
                lambda v: jnp.dot(v, ginv[s], precision=HI, preferred_element_type=jnp.float32)
            )
        if not last:
            inverse_copy(s + 1).wait_recv()
            inverse_relay(s + 1).start()
            block_copy(s + 1).wait_recv()
            cut(s + 1)
        for p in range(CHUNKS):
            sums[s][p].collect()
            if last:
                hand_over(s, p)
            update(s, p)
            if not last:
                product(s + 1, p, 1 - c)
                sums[s + 1][p].swap()
                product(s + 1, p, c)
                sums[s + 1][p].scatter()
                hand_over(s, p)
        if s > 1:
            for p in range(CHUNKS):
                coef_copy(s - 1, p).wait_recv()
                coef_relay(s - 1, p).start()

    def turn_back(i):
        at = pl.ds(pl.multiple_of(i * TILE, TILE), TILE)
        out_ref[:, at] = rest[at, :].T

    tiles(tg // TILE, turn_back)
    for p in range(CHUNKS):
        coef_copy(nb - 1, p).wait_recv()
        coef_relay(nb - 1, p).start()
    for s in range(1, nb):
        for copy in (block_copy, inverse_copy, inverse_relay):
            copy(s).wait_send()
        for p in range(CHUNKS):
            coef_relay(s, p).wait_recv()
            coef_copy(s, p).wait_send()
            coef_relay(s, p).wait_send()


def gathered(features, targets):
    nb, nrows = lax.axis_size("feat"), lax.axis_size("rows")
    height, width = features.shape
    tg = targets.shape[1]
    nz = nrows // 2
    chunk = tg // CHUNKS
    m = width // TILE
    packed = m * (m + 1) // 2 * TILE
    f32 = jnp.float32
    sums = 1 + nb * CHUNKS
    vmem = pl.BlockSpec(memory_space=pltpu.VMEM)
    dma = pltpu.SemaphoreType.DMA
    return pl.pallas_call(
        functools.partial(sweep_kernel, nb, nrows),
        out_shape=(
            jax.ShapeDtypeStruct((width, tg * nb), f32),
            jax.ShapeDtypeStruct((height, tg), f32),
        ),
        in_specs=[vmem] * 2,
        out_specs=(vmem, vmem),
        scratch_shapes=[
            pltpu.VMEM((nb - 1, height, width), f32),
            pltpu.VMEM((2, height, width), jnp.bfloat16),
            pltpu.VMEM((2, height, width), jnp.bfloat16),
            pltpu.VMEM((tg, height), f32),
            pltpu.VMEM((nb, width, width), f32),
            pltpu.VMEM((CHUNKS, chunk, width), f32),
            pltpu.VMEM((TILE, height), f32),
            pltpu.VMEM((packed, TILE), f32),
            pltpu.VMEM((packed // 2, TILE), f32),
            pltpu.VMEM((nz - 1, packed // nrows, TILE), f32),
            pltpu.VMEM((packed, TILE), f32),
            pltpu.VMEM((width, width), f32),
            pltpu.VMEM((nb, CHUNKS, chunk // 2, width), f32),
            pltpu.VMEM((nb, CHUNKS, nz - 1, chunk // nrows, width), f32),
            pltpu.VMEM((nb, CHUNKS, chunk, width), f32),
            pltpu.VMEM((nb - 1, CHUNKS, width // 2, chunk), f32),
            dma((2, nb - 1)),
            dma((2, sums)),
            dma((2, sums, nz - 1)),
            dma((2, sums, nz - 1)),
            dma((2, sums, nz)),
            dma((2, nb - 1)),
            dma((2, nb - 1)),
            dma((2, nb - 1, CHUNKS)),
            dma((2, nb - 1, CHUNKS)),
        ],
        compiler_params=pltpu.CompilerParams(collective_id=0, has_side_effects=True),
    )(features, targets)


def general(features, targets):
    nblocks = lax.axis_size("feat")
    owner = lax.axis_index("feat")
    width = features.shape[1]
    group_width = targets.shape[1]
    inverse = invert(lax.psum(tmul(features, features, HI), "rows"))
    coef = jnp.zeros((width, group_width * nblocks), jnp.float32)

    def section(s, carry):
        coef, res = carry
        group = (owner - s) % nblocks
        product = tmul(features, res, HI)
        share = lax.psum_scatter(product, "rows", scatter_dimension=1, tiled=True)
        part = jnp.dot(inverse, share, precision=HI, preferred_element_type=jnp.float32)
        step = lax.all_gather(part, "rows", axis=1, tiled=True)
        start = group * group_width
        old = lax.dynamic_slice_in_dim(coef, start, group_width, 1)
        coef = lax.dynamic_update_slice_in_dim(coef, old + step, start, 1)
        res = res - jnp.dot(features, step, precision=HI, preferred_element_type=jnp.float32)
        res = shifted(res, "feat", 1)
        return (coef, res)

    return lax.fori_loop(0, SWEEPS * nblocks, section, (coef, targets))


def on_device(features, targets):
    nblocks = lax.axis_size("feat")
    nrows = lax.axis_size("rows")
    width, group_width = features.shape[1], targets.shape[1]
    fits = nblocks > 1 and nblocks * features.size * 4 <= GATHER_BYTES
    whole = nrows % 2 == 0 and nrows > 2 and features.shape[0] % 128 == 0
    packed = (width // TILE) * (width // TILE + 1) // 2 * TILE
    even = width % (2 * TILE) == 0 and packed % (8 * nrows) == 0
    even = even and group_width % (CHUNKS * max(TILE, 8 * nrows)) == 0
    if SWEEPS == 1 and fits and whole and even:
        return gathered(features, targets)
    return general(features, targets)


def solution(mesh):
    return jax.shard_map(
        on_device,
        mesh=mesh,
        in_specs=(P("rows", "feat"), P("rows", "feat")),
        out_specs=(P("feat", None), P("rows", "feat")),
        check_vma=False,
    )
```

```python
import functools

import jax
import jax.numpy as jnp
from jax import lax
from jax.experimental import pallas as pl
from jax.experimental.pallas import tpu as pltpu
from jax.sharding import PartitionSpec as P

SWEEPS = 1
HI = lax.Precision.HIGHEST
GATHER_BYTES = 16 * 2**20


def shifted(block, axis, distance):
    devices = range(lax.axis_size(axis))
    route = [((i - distance) % len(devices), i) for i in devices]
    return lax.ppermute(block, axis, route)


def invert_tile(m):
    n = m.shape[0]
    lane = lax.broadcasted_iota(jnp.int32, (8, n), 1)
    sub = lax.broadcasted_iota(jnp.int32, (8, n), 0)
    lanes = lax.broadcasted_iota(jnp.int32, (n, n), 1)
    for q in range(n // 8):
        c = 8 * q
        panel = m[c : c + 8, :]
        d = [jnp.broadcast_to(panel[:, c + t : c + t + 1], (8, n)) for t in range(8)]
        mine = (lane >= c) & (lane < c + 8)
        panel = jnp.where(mine, jnp.where(lane - c == sub, 1.0, 0.0), panel)
        for t in range(8):
            inv = 1.0 / d[t][t : t + 1, :]
            row = panel[t : t + 1, :] * inv
            panel = jnp.where(sub == t, row, panel - d[t] * row)
            for u in range(t + 1, 8):
                head = d[u][t : t + 1, :] * inv
                d[u] = jnp.where(sub == t, head, d[u] - d[t] * head)
        new = jnp.where((lanes >= c) & (lanes < c + 8), 0.0, m)
        for t in range(8):
            new = new - jnp.broadcast_to(m[:, c + t : c + t + 1], (n, n)) * panel[t : t + 1, :]
        parts = [new[:c, :]] if q else []
        parts.append(panel)
        if c + 8 < n:
            parts.append(new[c + 8 :, :])
        m = jnp.concatenate(parts, axis=0)
    return m


def invert_kernel(tile, a_ref, o_ref):
    n = a_ref.shape[0]
    o_ref[...] = a_ref[...]
    eye = jnp.where(
        lax.broadcasted_iota(jnp.int32, (tile, tile), 0)
        == lax.broadcasted_iota(jnp.int32, (tile, tile), 1),
        1.0,
        0.0,
    )

    def block(k, _):
        at = pl.ds(pl.multiple_of(k * tile, tile), tile)
        pivot = invert_tile(o_ref[at, at])
        column = o_ref[:, at]
        o_ref[at, at] = eye
        row = jnp.dot(pivot, o_ref[at, :], precision=HI, preferred_element_type=jnp.float32)
        o_ref[:, at] = jnp.zeros((n, tile), jnp.float32)
        o_ref[...] -= jnp.dot(column, row, precision=HI, preferred_element_type=jnp.float32)
        o_ref[at, :] = row
        return 0

    lax.fori_loop(0, n // tile, block, 0)


def invert(gram):
    n = gram.shape[0]
    return pl.pallas_call(
        functools.partial(invert_kernel, min(128, n)),
        out_shape=jax.ShapeDtypeStruct((n, n), jnp.float32),
        in_specs=[pl.BlockSpec(memory_space=pltpu.VMEM)],
        out_specs=pl.BlockSpec(memory_space=pltpu.VMEM),
        cost_estimate=pl.CostEstimate(
            flops=2 * n**3 * 20, bytes_accessed=8 * n * n, transcendentals=0
        ),
    )(gram)


def tmul(a, b, precision):
    return lax.dot_general(
        a, b, (((0,), (0,)), ((), ())), precision=precision, preferred_element_type=jnp.float32
    )


def split(x):
    high = x.astype(jnp.bfloat16)
    return high, (x - high.astype(jnp.float32)).astype(jnp.bfloat16)


def dot3(a, b, contract):
    dims = (contract, ((), ()))
    mul = functools.partial(
        lax.dot_general, dimension_numbers=dims, preferred_element_type=jnp.float32
    )
    rows = a[0].shape[0]
    both = mul(jnp.concatenate(a, axis=0), b[0])
    return both[:rows] + (both[rows:] + mul(a[0], b[1]))


class RowSum:
    def __init__(self, net, k, n, src, pair_buf, rs_buf, dst):
        self.net, self.k, self.src, self.dst = net, k, src, dst
        self.pair_buf, self.rs_buf = pair_buf, rs_buf
        self.half, self.size = n // 2, n // 2 // net.nz

    def slot(self, d):
        net = self.net
        return rows_of(net.c * self.half + ((net.z + d) % net.nz) * self.size, self.size)

    def pair_slot(self, d):
        return rows_of(((self.net.z + d) % self.net.nz) * self.size, self.size)

    def swap(self):
        net = self.net
        away = self.src.at[rows_of((1 - net.c) * self.half, self.half)]
        self.sends = [net.copy(away, self.pair_buf, net.psem, (self.k,), net.mate)]
        self.sends[0].start()

    def scatter(self):
        net = self.net
        self.sends[0].wait_recv()
        for d in range(1, net.nz):
            at = self.slot(d)
            self.src[at, :] += self.pair_buf[self.pair_slot(d), :]
            copy = net.copy(
                self.src.at[at], self.rs_buf.at[d - 1], net.rsem, (self.k, d - 1), net.along(d)
            )
            copy.start()
            self.sends.append(copy)

    def finish(self, apply):
        net = self.net
        total = self.src[self.slot(0), :] + self.pair_buf[self.pair_slot(0), :]
        for d in range(1, net.nz):
            self.sends[d].wait_recv()
            total = total + self.rs_buf[d - 1]
        own = self.dst.at[self.slot(0)]
        own[...] = apply(total)
        self.spread = []
        for d in range(1, net.nz):
            copy = net.copy(own, own, net.asem, (self.k, d - 1), net.along(d))
            copy.start()
            self.spread.append(copy)
        self.relay = [net.copy(own, own, net.wsem, (self.k, 0), net.mate)]
        self.relay[0].start()

    def collect(self):
        net = self.net
        for d in range(1, net.nz):
            self.spread[d - 1].wait_recv()
            piece = self.dst.at[self.slot(net.nz - d)]
            self.relay.append(net.copy(piece, piece, net.wsem, (self.k, d), net.mate))
            self.relay[d].start()
        for copy in self.relay:
            copy.wait_recv()
        for copy in self.sends + self.spread + self.relay:
            copy.wait_send()


class Net:
    def __init__(self, nb, nrows, psem, rsem, asem, wsem):
        self.nb, self.nz = nb, nrows // 2
        self.r, self.g = lax.axis_index("rows"), lax.axis_index("feat")
        self.z, self.c = self.r // 2, self.r % 2
        self.mate = (self.r + 1 - 2 * self.c, self.g)
        self.psem, self.rsem, self.asem, self.wsem = psem, rsem, asem, wsem

    def along(self, d):
        return (((self.z + d) % self.nz) * 2 + self.c, self.g)

    def owner_of(self, s):
        return (self.r, (self.g + s) % self.nb)

    def copy(self, src, dst, sems, at, device):
        return pltpu.make_async_remote_copy(
            src_ref=src, dst_ref=dst, send_sem=sems.at[(0,) + at], recv_sem=sems.at[(1,) + at],
            device_id=device, device_id_type=pl.DeviceIdType.MESH,
        )

    def greet(self):
        barrier = pltpu.get_barrier_semaphore()
        peers = [self.mate] + [self.along(d) for d in range(1, self.nz)]
        peers += [self.owner_of(s) for s in range(1, self.nb)]
        for peer in peers:
            pl.semaphore_signal(
                barrier, inc=1, device_id=peer, device_id_type=pl.DeviceIdType.MESH
            )
        pl.semaphore_wait(barrier, len(peers))


def rows_of(start, size):
    return pl.ds(pl.multiple_of(start, 8), size)


def tiles(count, body):
    lax.fori_loop(0, count, lambda i, _: (body(i), 0)[1], 0)


TILE = 128
CHUNKS = 2


def sweep_kernel(
    nb, nrows, x_ref, t_ref, coef_ref, out_ref,
    xbuf, xh, xl, rest, ginv, part, xt, gpart, gpair, grs, gsum, gfull, pairb, rsb, full, cbuf,
    fsem, psem, rsem, asem, wsem, isem, jsem, csem, dsem,
):
    net = Net(nb, nrows, psem, rsem, asem, wsem)
    c, g = net.c, net.g
    height, width = x_ref.shape
    tg = t_ref.shape[1]
    chunk = tg // CHUNKS
    net.greet()

    def block_copy(s):
        return net.copy(x_ref, xbuf.at[s - 1], fsem, (s - 1,), net.owner_of(nb - s))

    block_copy(1).start()

    m = width // TILE
    pairs = [(i, j) for i in range(m) for j in range(i + 1)]
    for i in range(m):
        xt[...] = x_ref[:, i * TILE : (i + 1) * TILE].T
        low = jnp.dot(
            xt[...], x_ref[:, : (i + 1) * TILE], precision=HI, preferred_element_type=jnp.float32
        )
        for j in range(i + 1):
            at = pairs.index((i, j)) * TILE
            gpart[at : at + TILE, :] = low[:, j * TILE : (j + 1) * TILE]
    gram = RowSum(net, 0, len(pairs) * TILE, gpart, gpair, grs, gsum)
    gram.swap()

    def turn(i):
        at = pl.ds(pl.multiple_of(i * TILE, TILE), TILE)
        rest[at, :] = t_ref[:, at].T

    def cut(s):
        block = xbuf.at[s - 1] if s else x_ref

        def body(i):
            at = pl.ds(pl.multiple_of(i * TILE, TILE), TILE)
            xh[s % 2, at, :], xl[s % 2, at, :] = split(block[at, :])

        tiles(height // TILE, body)

    sums = [
        [
            RowSum(
                net, 1 + s * CHUNKS + p, chunk, part.at[p], pairb.at[s, p], rsb.at[s, p],
                full.at[s, p],
            )
            for p in range(CHUNKS)
        ]
        for s in range(nb)
    ]

    def product(s, p):
        res = split(rest[p * chunk : (p + 1) * chunk, :])
        part[p] = dot3(res, (xh[s % 2], xl[s % 2]), ((1,), (0,)))

    def update(s, p):
        step = split(full[s, p])
        rest[p * chunk : (p + 1) * chunk, :] -= dot3(step, (xh[s % 2], xl[s % 2]), ((1,), (1,)))

    gram.scatter()
    tiles(tg // TILE, turn)
    cut(0)
    gram.finish(lambda v: v)
    for p in range(CHUNKS):
        product(0, p)
    gram.collect()
    if nb > 2:
        block_copy(2).start()
    for p in range(CHUNKS):
        sums[0][p].swap()
    for p in range(CHUNKS):
        sums[0][p].scatter()
    for at, (i, j) in enumerate(pairs):
        tile = gsum[at * TILE : (at + 1) * TILE, :]
        gfull[i * TILE : (i + 1) * TILE, j * TILE : (j + 1) * TILE] = tile
        if i != j:
            gfull[j * TILE : (j + 1) * TILE, i * TILE : (i + 1) * TILE] = tile.T
    invert_kernel(TILE, gfull, ginv.at[0])

    wh = width // 2
    mine = pl.ds(pl.multiple_of(c * wh, wh), wh)

    def inverse_copy(s):
        return net.copy(
            ginv.at[0, mine], ginv.at[s, mine], isem, (s - 1,), net.owner_of(nb - s)
        )

    def inverse_relay(s):
        return net.copy(ginv.at[s, mine], ginv.at[s, mine], jsem, (s - 1,), net.mate)

    for s in range(1, nb):
        inverse_copy(s).start()
    for s in range(3, nb):
        block_copy(s).start()

    def columns(group, p):
        return pl.ds(pl.multiple_of(group * tg + p * chunk, chunk), chunk)

    def coef_copy(s, p):
        return net.copy(
            cbuf.at[s - 1, p], coef_ref.at[mine, columns(g, p)], csem, (s - 1, p),
            net.owner_of(s),
        )

    def coef_relay(s, p):
        piece = coef_ref.at[mine, columns((g - s + nb) % nb, p)]
        return net.copy(piece, piece, dsem, (s - 1, p), net.mate)

    def hand_over(s, p):
        if s:
            cbuf[s - 1, p] = full[s, p, :, mine].T
            coef_copy(s, p).start()
        else:
            coef_ref[:, columns(g, p)] = full[s, p].T

    for s in range(nb):
        last = s + 1 == nb
        if s:
            inverse_relay(s).wait_recv()
        for p in range(CHUNKS):
            sums[s][p].finish(
                lambda v: jnp.dot(v, ginv[s], precision=HI, preferred_element_type=jnp.float32)
            )
        if not last:
            inverse_copy(s + 1).wait_recv()
            inverse_relay(s + 1).start()
            block_copy(s + 1).wait_recv()
            cut(s + 1)
        for p in range(CHUNKS):
            sums[s][p].collect()
            if last:
                hand_over(s, p)
            update(s, p)
            if not last:
                product(s + 1, p)
                sums[s + 1][p].swap()
                sums[s + 1][p].scatter()
                hand_over(s, p)
        if s > 1:
            for p in range(CHUNKS):
                coef_copy(s - 1, p).wait_recv()
                coef_relay(s - 1, p).start()

    def turn_back(i):
        at = pl.ds(pl.multiple_of(i * TILE, TILE), TILE)
        out_ref[:, at] = rest[at, :].T

    tiles(tg // TILE, turn_back)
    for p in range(CHUNKS):
        coef_copy(nb - 1, p).wait_recv()
        coef_relay(nb - 1, p).start()
    for s in range(1, nb):
        for copy in (block_copy, inverse_copy, inverse_relay):
            copy(s).wait_send()
        for p in range(CHUNKS):
            coef_relay(s, p).wait_recv()
            coef_copy(s, p).wait_send()
            coef_relay(s, p).wait_send()


def gathered(features, targets):
    nb, nrows = lax.axis_size("feat"), lax.axis_size("rows")
    height, width = features.shape
    tg = targets.shape[1]
    nz = nrows // 2
    chunk = tg // CHUNKS
    m = width // TILE
    packed = m * (m + 1) // 2 * TILE
    f32 = jnp.float32
    sums = 1 + nb * CHUNKS
    vmem = pl.BlockSpec(memory_space=pltpu.VMEM)
    dma = pltpu.SemaphoreType.DMA
    return pl.pallas_call(
        functools.partial(sweep_kernel, nb, nrows),
        out_shape=(
            jax.ShapeDtypeStruct((width, tg * nb), f32),
            jax.ShapeDtypeStruct((height, tg), f32),
        ),
        in_specs=[vmem] * 2,
        out_specs=(vmem, vmem),
        scratch_shapes=[
            pltpu.VMEM((nb - 1, height, width), f32),
            pltpu.VMEM((2, height, width), jnp.bfloat16),
            pltpu.VMEM((2, height, width), jnp.bfloat16),
            pltpu.VMEM((tg, height), f32),
            pltpu.VMEM((nb, width, width), f32),
            pltpu.VMEM((CHUNKS, chunk, width), f32),
            pltpu.VMEM((TILE, height), f32),
            pltpu.VMEM((packed, TILE), f32),
            pltpu.VMEM((packed // 2, TILE), f32),
            pltpu.VMEM((nz - 1, packed // nrows, TILE), f32),
            pltpu.VMEM((packed, TILE), f32),
            pltpu.VMEM((width, width), f32),
            pltpu.VMEM((nb, CHUNKS, chunk // 2, width), f32),
            pltpu.VMEM((nb, CHUNKS, nz - 1, chunk // nrows, width), f32),
            pltpu.VMEM((nb, CHUNKS, chunk, width), f32),
            pltpu.VMEM((nb - 1, CHUNKS, width // 2, chunk), f32),
            dma((2, nb - 1)),
            dma((2, sums)),
            dma((2, sums, nz - 1)),
            dma((2, sums, nz - 1)),
            dma((2, sums, nz)),
            dma((2, nb - 1)),
            dma((2, nb - 1)),
            dma((2, nb - 1, CHUNKS)),
            dma((2, nb - 1, CHUNKS)),
        ],
        compiler_params=pltpu.CompilerParams(collective_id=0, has_side_effects=True),
    )(features, targets)


def general(features, targets):
    nblocks = lax.axis_size("feat")
    owner = lax.axis_index("feat")
    width = features.shape[1]
    group_width = targets.shape[1]
    inverse = invert(lax.psum(tmul(features, features, HI), "rows"))
    coef = jnp.zeros((width, group_width * nblocks), jnp.float32)

    def section(s, carry):
        coef, res = carry
        group = (owner - s) % nblocks
        product = tmul(features, res, HI)
        share = lax.psum_scatter(product, "rows", scatter_dimension=1, tiled=True)
        part = jnp.dot(inverse, share, precision=HI, preferred_element_type=jnp.float32)
        step = lax.all_gather(part, "rows", axis=1, tiled=True)
        start = group * group_width
        old = lax.dynamic_slice_in_dim(coef, start, group_width, 1)
        coef = lax.dynamic_update_slice_in_dim(coef, old + step, start, 1)
        res = res - jnp.dot(features, step, precision=HI, preferred_element_type=jnp.float32)
        res = shifted(res, "feat", 1)
        return (coef, res)

    return lax.fori_loop(0, SWEEPS * nblocks, section, (coef, targets))


def on_device(features, targets):
    nblocks = lax.axis_size("feat")
    nrows = lax.axis_size("rows")
    width, group_width = features.shape[1], targets.shape[1]
    fits = nblocks > 1 and nblocks * features.size * 4 <= GATHER_BYTES
    whole = nrows % 2 == 0 and nrows > 2 and features.shape[0] % 128 == 0
    packed = (width // TILE) * (width // TILE + 1) // 2 * TILE
    even = width % (2 * TILE) == 0 and packed % (8 * nrows) == 0
    even = even and group_width % (CHUNKS * max(TILE, 8 * nrows)) == 0
    if SWEEPS == 1 and fits and whole and even:
        return gathered(features, targets)
    return general(features, targets)


def solution(mesh):
    return jax.shard_map(
        on_device,
        mesh=mesh,
        in_specs=(P("rows", "feat"), P("rows", "feat")),
        out_specs=(P("feat", None), P("rows", "feat")),
        check_vma=False,
    )
```
